128 devices in a mesh: rows: 32 (over x, z, y_lo), cols: 4 (over y_hi, core).
Axes of the slice: x: 4, y: 4 (y_hi: 2, y_lo: 2; y = y_hi * 2 + y_lo), z: 4, core: 2. Of those that a mesh axis runs over, the one named last changes fastest.
Arguments:
- vectors: bfloat16 [131072, 1024], P('rows'), may hold values from -6 to 6
- near_tiles: bfloat16 [512, 16, 256, 256], P(('rows', 'cols')), may hold values from -0.09375 to 0.09375
- near_cols: int32 [512, 16], P(('rows', 'cols')), may hold values from 0 to 19, as said below
- left_one: bfloat16 [131072, 512], P('rows', 'cols'), may hold values from -0.25 to 0.25
- right_one: bfloat16 [131072, 512], P('rows', 'cols'), may hold values from -0.0234375 to 0.0234375
- left_two: bfloat16 [131072, 512], P('rows', 'cols'), may hold values from -0.25 to 0.25
- right_two: bfloat16 [131072, 512], P('rows', 'cols'), may hold values from -0.03125 to 0.03125
Outputs:
- product: bfloat16 [131072, 1024], P(('rows', 'cols'))
The draws below stay inside these ranges and needn't reach their ends.
Inputs may be any that keep to these rules, and one draw needn't show every extreme that they name: `near_cols`: each row names 16 different column tiles of its window of 20.
All inputs are finite; a program needn't handle non-finite values.
Results may differ from the reference program's by a relative error of at most 0.014.
Values may be sent and summed in bfloat16 or wider, within the bound.
A program may use at most 192 MiB of HBM per device.

```python
import jax
import jax.numpy as jnp
from jax import lax

B = 256
R = 512
NRHS = 1024
TILES_DEV = 16
NNZ = 16
REACH = 2
WINDOW = 20
NT = 512
NR = 131072
N_ROWS = 32


def draw_near_cols(key, part):
    scores = jax.random.randint(key, (NT, WINDOW), 0, 1 << 30)
    ranking = jnp.argsort(scores, axis=1, stable=True)
    return ranking[:, :NNZ].astype(jnp.int32)


def levels(stream_key, dims, cuts, low, top_value):
    loudness, own = 1.0, jax.random.fold_in(stream_key, 6)
    for position, parts in cuts:
        steps = jnp.exp(jax.random.uniform(jax.random.fold_in(own, position), (parts,), jnp.float32, low / len(cuts), top_value / len(cuts)))
        loudness = loudness * jnp.repeat(steps, dims[position] // parts).reshape([-1 if axis == position else 1 for axis in range(len(dims))])
    return loudness


def gaussian(own_key, shape, width, most, pieces=(), kind=jnp.bfloat16):
    array = jax.random.normal(own_key, shape, jnp.float32) * width
    if len(pieces) > 0:
        array = levels(own_key, shape, pieces, -0.22, 0.18) * array
    return jnp.clip(array, min=-most, max=most).astype(kind)


def setup_inputs(seed: int = 0) -> dict:
    key_list = jax.random.split(jax.random.key(seed), 8)
    return {
        "vectors": gaussian(key_list[0], (NR, NRHS), 1.0, 6.0, ((0, 32),)),
        "near_tiles": gaussian(key_list[1], (NT, NNZ, B, B), (NNZ * B) ** -0.5, 0.09375, ((0, 128),)),
        "near_cols": draw_near_cols(jax.random.fold_in(key_list[7], 71), 0),
        "left_one": gaussian(key_list[3], (NR, R), R ** -0.5, 0.25, ((0, 32), (1, 4))),
        "right_one": gaussian(key_list[4], (NR, R), (NR // 2) ** -0.5, 0.0234375, ((0, 32), (1, 4))),
        "left_two": gaussian(key_list[5], (NR, R), R ** -0.5, 0.25, ((0, 32), (1, 4))),
        "right_two": gaussian(key_list[6], (NR, R), (NR // 4) ** -0.5, 0.03125, ((0, 32), (1, 4))),
    }


def near_range(padded, near_tiles, near_cols, range_index):
    begin = (range_index * TILES_DEV * B).astype(jnp.int32)
    window_rows = lax.dynamic_slice_in_dim(padded, begin, WINDOW * B, 0)
    blocks = window_rows.reshape(WINDOW, B, NRHS)
    leading_tile = (range_index * TILES_DEV).astype(jnp.int32)
    tiles_here = lax.dynamic_slice_in_dim(near_tiles, leading_tile, TILES_DEV, 0).astype(jnp.float32)
    cols_here = lax.dynamic_slice_in_dim(near_cols, leading_tile, TILES_DEV, 0)
    picked = blocks[cols_here]
    result = jnp.einsum("tkab,tkbn->tan", tiles_here, picked, precision=lax.Precision.HIGHEST)
    return result.reshape(TILES_DEV * B, NRHS)


def coupling(vectors_wide, left, right, groups):
    group_rows = NR // groups
    right_vector_sets = right.astype(jnp.float32).reshape(groups, group_rows, R)
    vector_sets = vectors_wide.reshape(groups, group_rows, NRHS)
    running_sums = jnp.einsum("qwh,qwp->qhp", right_vector_sets, vector_sets, precision=lax.Precision.HIGHEST)
    partner_index = running_sums.reshape(groups // 2, 2, R, NRHS)[:, ::-1].reshape(groups, R, NRHS)
    partner_index = lax.optimization_barrier(partner_index.astype(jnp.bfloat16)).astype(jnp.float32)
    left_vector_sets = left.astype(jnp.float32).reshape(groups, group_rows, R)
    coupled_result = jnp.einsum("dzl,dlk->dzk", left_vector_sets, partner_index, precision=lax.Precision.HIGHEST)
    return coupled_result.reshape(NR, NRHS)


def reference(vectors, near_tiles, near_cols, left_one, right_one, left_two, right_two):
    vectors_wide = vectors.astype(jnp.float32)
    padded = jnp.pad(vectors_wide, ((REACH * B, REACH * B), (0, 0)))
    near = lax.map(lambda index: near_range(padded, near_tiles, near_cols, index), jnp.arange(N_ROWS, dtype=jnp.int32))
    near = near.reshape(NR, NRHS)
    total = near + coupling(vectors_wide, left_one, right_one, 2) + coupling(vectors_wide, left_two, right_two, 4)
    return total.astype(jnp.bfloat16)
```

```python
import jax
import jax.numpy as jnp
from jax import lax
from jax.experimental import pallas as pl
from jax.experimental.pallas import tpu as pltpu
from jax.sharding import PartitionSpec as P

B = 256
REACH = 2
NNZ = 16
TILES = 4
OWN = 16
WINDOW = OWN + 2 * REACH
M = OWN * B
N = 1024
HALO = REACH * B
QUARTER = HALO // 4
ROWS = TILES * B
RB = 128
HALF = ROWS // 2
BF = jnp.bfloat16
F32 = jnp.float32


def kernel(
    inv,
    vec,
    near,
    left_one,
    left_two,
    right_one,
    right_two,
    out,
    win,
    nt,
    dense,
    rt,
    pacc,
    part,
    zin,
    ysend,
    yin,
    keep,
    xsend,
    xin,
    coeff,
    left,
    relay,
    acc,
    vec_sem,
    loc_sem,
    hop_s,
    hop_r,
    fwd_s,
    fwd_r,
    swap_s,
    swap_r,
    halo_s,
    halo_r,
    share_s,
    share_r,
    z_s,
    z_r,
    y_s,
    y_r,
    x_s,
    x_r,
    g_s,
    g_r,
    ring_s,
    ring_r,
    core_s,
    core_r,
):
    lefts = (left_one, left_two)
    r = lax.axis_index("rows")
    c = lax.axis_index("cols")
    x = r // 8
    z = (r // 2) % 4
    yl = r % 2
    yh = c // 2
    k = c % 2
    flip = r + 1 - 2 * yl
    oh = 1 - yh
    ok = 1 - k
    highs = (yh, oh)

    def dev(row, high, core):
        return (row, high * 2 + core)

    def at_z(zz):
        return x * 8 + zz * 2 + yl

    def at_x(xx):
        return xx * 8 + z * 2 + yl

    zp = (z + 1) % 4
    zm = (z + 3) % 4
    zo = (z + 2) % 4
    x1 = x + 1 - 2 * (x % 2)
    x2 = (x + 2) % 4
    x3 = 3 - x
    xpar = x % 2
    up = (r + 1) % 32
    down = (r + 31) % 32
    other = dev(r, yh, ok)

    def rcopy(src, dst, send, recv, target):
        return pltpu.make_async_remote_copy(
            src_ref=src,
            dst_ref=dst,
            send_sem=send,
            recv_sem=recv,
            device_id=target,
            device_id_type=pl.DeviceIdType.MESH,
        )

    steps = 4
    rows = M // steps
    vec_in = [
        pltpu.make_async_copy(
            vec.at[pl.ds(i * rows, rows)], win.at[pl.ds(HALO + i * rows, rows)], vec_sem.at[i]
        )
        for i in range(steps)
    ]
    right_in = [
        pltpu.make_async_copy(right_one, rt.at[:, pl.ds(0, RB)], loc_sem.at[0]),
        pltpu.make_async_copy(right_two, rt.at[:, pl.ds(RB, RB)], loc_sem.at[1]),
    ]
    near_in = pltpu.make_async_copy(near, nt.at[:, pl.ds(0, NNZ)], loc_sem.at[2])
    left_in = [
        pltpu.make_async_copy(
            lefts[l].at[pl.ds(c * ROWS, ROWS)], left.at[k, l, yh], loc_sem.at[3 + l]
        )
        for l in range(2)
    ]
    for copy in right_in + vec_in + [near_in] + left_in:
        copy.start()

    barrier = pltpu.get_barrier_semaphore()
    partners = [
        dev(up, yh, k),
        dev(up, oh, k),
        dev(down, yh, k),
        dev(down, oh, k),
        dev(flip, yh, ok),
        dev(flip, oh, ok),
        dev(r, oh, k),
        other,
        dev(at_z(zp), yh, k),
        dev(at_z(zm), yh, k),
        dev(at_z(zo), yh, k),
        dev(at_x(x1), yh, k),
        dev(at_x(x2), yh, k),
        dev(at_x(x3), yh, k),
    ]
    for partner in partners:
        pl.semaphore_signal(
            barrier, inc=1, device_id=partner, device_id_type=pl.DeviceIdType.MESH
        )
    pl.semaphore_wait(barrier, len(partners))

    hops = {}
    forwards = {}
    for p in range(2):
        for core in range(2):
            for l in range(2):
                hops[p, core, l] = rcopy(
                    lefts[l].at[pl.ds((oh * 2 + core) * ROWS + p * HALF, HALF)],
                    relay.at[p, core, l],
                    hop_s.at[p, core, l],
                    hop_r.at[p, core, l],
                    dev(flip, highs[p], k),
                )
                forwards[p, core, l] = rcopy(
                    relay.at[p, core, l],
                    left.at[k, l, highs[p], pl.ds(p * HALF, HALF)],
                    fwd_s.at[p, core, l],
                    fwd_r.at[p, k, l],
                    dev(flip, highs[1 - p], core),
                )
    arrivals = {
        (p, core, l): rcopy(
            relay.at[p, core, l],
            left.at[core, l, oh, pl.ds(p * HALF, HALF)],
            fwd_s.at[p, core, l],
            fwd_r.at[p, core, l],
            dev(flip, highs[p], core),
        )
        for p in range(2)
        for core in range(2)
        for l in range(2)
    }
    swaps = [
        rcopy(
            lefts[l].at[pl.ds((yh * 2 + ok) * ROWS, ROWS)],
            left.at[k, l, yh],
            swap_s.at[l],
            swap_r.at[l],
            other,
        )
        for l in range(2)
    ]
    for core in range(2):
        for l in range(2):
            for p in range(2):
                hops[p, core, l].start()
    for copy in swaps:
        copy.start()

    for copy in right_in:
        copy.wait()
    for i in range(steps):
        vec_in[i].wait()
        term = lax.dot_general(
            rt[pl.ds(i * rows, rows), :],
            win[pl.ds(HALO + i * rows, rows), :],
            (((0,), (0,)), ((), ())),
            preferred_element_type=F32,
        )
        if i == 0:
            pacc[...] = term
        else:
            pacc[...] += term
    for l in range(2):
        for zz in range(4):
            part[zz, l] = pacc[pl.ds(l * RB + zz * 32, 32), :].astype(BF)
    targets = (zp, zo, zm)
    z_out = [
        rcopy(
            part.at[targets[j]],
            zin.at[z],
            z_s.at[j],
            z_r.at[j],
            dev(at_z(targets[j]), yh, k),
        )
        for j in range(3)
    ]
    for j in (1, 0, 2):
        z_out[j].start()

    nt[:, NNZ] = jnp.zeros((TILES, B, B), BF)
    near_in.wait()

    def assemble(w, carry):
        for t in range(TILES):
            dense[pl.ds(t * B, B), pl.ds(pl.multiple_of(w * B, B), B)] = nt[t, inv[t, w]]
        return carry

    lax.fori_loop(0, WINDOW, assemble, 0)

    def near_part(first, depth, initial=False):
        def columns(i, carry):
            cols = pl.ds(pl.multiple_of(i * B, B), B)
            term = jnp.dot(
                dense[:, pl.ds(first, depth)],
                win[pl.ds(first, depth), cols],
                preferred_element_type=F32,
            )
            if initial:
                acc[:, cols] = term
            else:
                acc[:, cols] += term
            return carry

        lax.fori_loop(0, N // B, columns, 0)

    near_part(HALO, 1024, True)

    for copy in z_out:
        copy.wait_recv()
    for l in range(2):
        base = pl.multiple_of(l * RB + z * 32, 32)
        total = pacc[pl.ds(base, 32), :]
        for j in range(1, 4):
            total = total + zin[(z + j) % 4, l].astype(F32)
        pacc[pl.ds(base, 32), :] = total
        keep[l] = pacc[pl.ds(pl.multiple_of(base + yl * 16, 16), 16), :]
        ysend[l] = pacc[pl.ds(pl.multiple_of(base + (1 - yl) * 16, 16), 16), :].astype(BF)
    y_out = rcopy(ysend, yin, y_s.at[0], y_r.at[0], dev(flip, yh, k))
    y_out.start()

    halos = {}
    shares = {}
    for d in range(2):
        for p in range(2):
            quarter = (2 * p + k) * QUARTER
            source = quarter + (M - HALO if d == 0 else 0)
            place = win.at[pl.ds(quarter + (0 if d == 0 else HALO + M), QUARTER)]
            halos[d, p] = rcopy(
                vec.at[pl.ds(source, QUARTER)],
                place,
                halo_s.at[d, p],
                halo_r.at[d, p],
                dev(up if d == 0 else down, highs[p], k),
            )
            shares[d, p] = rcopy(place, place, share_s.at[d, p], share_r.at[d, p], other)
    sends = (r < 31, r > 0)
    gets = (r > 0, r < 31)

    def halo_start(d):
        @pl.when(sends[d])
        def _():
            for p in range(2):
                halos[d, p].start()

    def halo_share(d):
        @pl.when(gets[d])
        def _():
            for p in range(2):
                halos[d, p].wait_recv()
                shares[d, p].start()

        @pl.when(jnp.logical_not(gets[d]))
        def _():
            win[pl.ds(0 if d == 0 else HALO + M, HALO), :] = jnp.zeros((HALO, N), BF)

    def halo_wait(d):
        @pl.when(gets[d])
        def _():
            for p in range(2):
                shares[d, p].wait()

        @pl.when(sends[d])
        def _():
            for p in range(2):
                halos[d, p].wait_send()

    halo_start(0)
    near_part(HALO + 1024, 1024)

    y_out.wait()
    for l in range(2):
        xsend[l] = (keep[l] + yin[l].astype(F32)).astype(BF)
    x_out = [
        rcopy(
            xsend.at[1], coeff.at[k, 1, yh, z, yl], x_s.at[0], x_r.at[0], dev(at_x(x1), yh, k)
        ),
        rcopy(xsend.at[0], xin.at[xpar], x_s.at[1], x_r.at[1], dev(at_x(x2), yh, k)),
        rcopy(xsend.at[0], xin.at[xpar], x_s.at[2], x_r.at[2], dev(at_x(x3), yh, k)),
    ]
    for copy in x_out:
        copy.start()
    near_part(HALO + 2048, 1024)
    for copy in x_out:
        copy.wait()
    coeff[k, 0, yh, z, yl] = (xin[0].astype(F32) + xin[1].astype(F32)).astype(BF)

    mine = coeff.at[k, :, yh, z, yl]
    g_out = [
        rcopy(mine, mine, g_s.at[i], g_r.at[i], target)
        for i, target in enumerate((dev(flip, yh, k), dev(flip, oh, k), dev(r, oh, k)))
    ]
    for i in (2, 0, 1):
        g_out[i].start()
    halo_start(1)
    for core in range(2):
        for l in range(2):
            for p in range(2):
                hops[p, core, l].wait_recv()
                forwards[p, core, l].start()
    near_part(HALO + 3072, 1024)
    for copy in g_out:
        copy.wait()

    def at(zz):
        return coeff.at[k, :, :, zz]

    def level(l, zz):
        return coeff.at[k, l, :, zz]

    ring = [
        rcopy(at(z), at(z), ring_s.at[0], ring_r.at[0], dev(at_z(zp), yh, k)),
        rcopy(at(z), at(z), ring_s.at[1], ring_r.at[1], dev(at_z(zm), yh, k)),
        rcopy(level(0, zm), level(0, zm), ring_s.at[2], ring_r.at[2], dev(at_z(zp), yh, k)),
        rcopy(level(1, zp), level(1, zp), ring_s.at[3], ring_r.at[3], dev(at_z(zm), yh, k)),
    ]
    cores = [
        rcopy(part_, part_, core_s.at[i], core_r.at[i], other)
        for i, part_ in enumerate((at(z), at(zm), at(zp), level(0, zo), level(1, zo)))
    ]
    ring[0].start()
    ring[1].start()
    cores[0].start()
    halo_share(0)
    for i in range(2):
        ring[i].wait_recv()
        ring[i + 2].start()
        cores[i + 1].start()
    halo_wait(0)
    near_part(0, HALO)
    for i in range(2):
        ring[i + 2].wait_recv()
        cores[i + 3].start()
    halo_share(1)
    halo_wait(1)
    near_part(HALO + M, HALO)

    for copy in cores + swaps:
        copy.wait()
    for copy in left_in:
        copy.wait()
    for p in range(2):
        for core in range(2):
            for l in range(2):
                arrivals[p, core, l].wait_recv()
        here = pl.ds(p * HALF, HALF)

        def columns(i, carry):
            cols = pl.ds(pl.multiple_of(i * B, B), B)
            basis = jnp.concatenate(
                [left[a, b, h, here, :] for a in range(2) for b in range(2) for h in range(2)],
                axis=1,
            )
            far = jnp.dot(
                basis, coeff[..., cols].reshape(8 * RB, B), preferred_element_type=F32
            )
            out[here, cols] = (acc[here, cols] + far).astype(out.dtype)
            return carry

        lax.fori_loop(0, N // B, columns, 0)

    for copy in list(hops.values()) + list(forwards.values()) + z_out + ring:
        copy.wait_send()


def per_device(vectors, near_tiles, near_cols, left_one, right_one, left_two, right_two):
    named = near_cols[:, :, None] == jnp.arange(WINDOW, dtype=jnp.int32)
    order = jnp.arange(NNZ, dtype=jnp.int32)[None, :, None] - NNZ
    inv = NNZ + jnp.sum(jnp.where(named, order, 0), axis=1).astype(jnp.int32)
    dma = pltpu.SemaphoreType.DMA
    hbm = pl.BlockSpec(memory_space=pltpu.HBM)
    return pl.pallas_call(
        kernel,
        out_shape=jax.ShapeDtypeStruct((ROWS, N), BF),
        in_specs=[pl.BlockSpec(memory_space=pltpu.SMEM)] + [hbm] * 6,
        out_specs=pl.BlockSpec(memory_space=pltpu.VMEM),
        scratch_shapes=[
            pltpu.VMEM((WINDOW * B, N), BF),
            pltpu.VMEM((TILES, NNZ + 1, B, B), BF),
            pltpu.VMEM((ROWS, WINDOW * B), BF),
            pltpu.VMEM((M, 2 * RB), BF),
            pltpu.VMEM((2 * RB, N), F32),
            pltpu.VMEM((4, 2, 32, N), BF),
            pltpu.VMEM((4, 2, 32, N), BF),
            pltpu.VMEM((2, 16, N), BF),
            pltpu.VMEM((2, 16, N), BF),
            pltpu.VMEM((2, 16, N), F32),
            pltpu.VMEM((2, 16, N), BF),
            pltpu.VMEM((2, 16, N), BF),
            pltpu.VMEM((2, 2, 2, 4, 2, 16, N), BF),
            pltpu.VMEM((2, 2, 2, ROWS, RB), BF),
            pltpu.VMEM((2, 2, 2, HALF, RB), BF),
            pltpu.VMEM((ROWS, N), F32),
            dma((4,)),
            dma((5,)),
            dma((2, 2, 2)),
            dma((2, 2, 2)),
            dma((2, 2, 2)),
            dma((2, 2, 2)),
            dma((2,)),
            dma((2,)),
            dma((2, 2)),
            dma((2, 2)),
            dma((2, 2)),
            dma((2, 2)),
            dma((3,)),
            dma((3,)),
            dma((1,)),
            dma((1,)),
            dma((3,)),
            dma((3,)),
            dma((3,)),
            dma((3,)),
            dma((4,)),
            dma((4,)),
            dma((5,)),
            dma((5,)),
        ],
        compiler_params=pltpu.CompilerParams(
            collective_id=0, has_side_effects=True, vmem_limit_bytes=56 * 1024 * 1024
        ),
    )(inv, vectors, near_tiles, left_one, left_two, right_one, right_two)


def solution(mesh):
    placed = (
        P("rows", None),
        P(("rows", "cols"), None, None, None),
        P(("rows", "cols"), None),
        P("rows", "cols"),
        P("rows", "cols"),
        P("rows", "cols"),
        P("rows", "cols"),
    )
    return jax.shard_map(
        per_device, mesh=mesh, in_specs=placed, out_specs=P(("rows", "cols"), None), check_vma=False
    )
```

```python
import jax
import jax.numpy as jnp
from jax import lax
from jax.experimental import pallas as pl
from jax.experimental.pallas import tpu as pltpu
from jax.sharding import PartitionSpec as P

B = 256
REACH = 2
NNZ = 16
TILES = 4
OWN = 16
WINDOW = OWN + 2 * REACH
M = OWN * B
N = 1024
HALO = REACH * B
QUARTER = HALO // 4
ROWS = TILES * B
RB = 128
HALF = ROWS // 2
PIECE = HALF // 2
STEPS = 8
EARLY = 4
FIRST = 5
PLAN = (2, 4, 4, 4)
BF = jnp.bfloat16
F32 = jnp.float32


def kernel(
    cols,
    vec,
    near,
    left_one,
    left_two,
    right_one,
    right_two,
    out,
    win,
    nt,
    dense,
    rt,
    pacc,
    part,
    zin,
    zrelay,
    ysend,
    yin,
    keep,
    xsend,
    xin,
    coeff,
    left,
    relay,
    far_rows,
    acc,
    vec_sem,
    right_sem,
    loc_sem,
    hop_s,
    hop_r,
    fwd_s,
    fwd_r,
    swap_s,
    swap_r,
    far_s,
    far_r,
    near_s,
    near_r,
    halo_s,
    halo_r,
    share_s,
    share_r,
    z_s,
    z_r,
    y_s,
    y_r,
    x_s,
    x_r,
    g_s,
    g_r,
    ring_s,
    ring_r,
    core_s,
    core_r,
):
    lefts = (left_one, left_two)
    rights = (right_one, right_two)
    r = lax.axis_index("rows")
    c = lax.axis_index("cols")
    x = r // 8
    z = (r // 2) % 4
    yl = r % 2
    yh = c // 2
    k = c % 2
    flip = r + 1 - 2 * yl
    oh = 1 - yh
    ok = 1 - k
    highs = (yh, oh)

    def dev(row, high, core):
        return (row, high * 2 + core)

    def at_z(zz):
        return x * 8 + zz * 2 + yl

    def at_x(xx):
        return xx * 8 + z * 2 + yl

    zp = (z + 1) % 4
    zm = (z + 3) % 4
    zo = (z + 2) % 4
    x1 = x + 1 - 2 * (x % 2)
    x2 = (x + 2) % 4
    x3 = 3 - x
    xpar = x % 2
    other = dev(r, yh, ok)

    def rcopy(src, dst, send, recv, target):
        return pltpu.make_async_remote_copy(
            src_ref=src,
            dst_ref=dst,
            send_sem=send,
            recv_sem=recv,
            device_id=target,
            device_id_type=pl.DeviceIdType.MESH,
        )

    barrier = pltpu.get_barrier_semaphore()
    partners = [
        dev(flip, yh, k),
        dev(flip, oh, k),
        dev(flip, yh, ok),
        dev(flip, oh, ok),
        dev(r, oh, k),
        other,
        dev(at_z(zp), yh, k),
        dev(at_z(zm), yh, k),
        dev(at_x(x1), yh, k),
        dev(at_x(x2), yh, k),
        dev(at_x(x3), yh, k),
        dev((r + 2) % 32, yh, k),
        dev((r + 30) % 32, yh, k),
    ]
    for partner in partners:
        pl.semaphore_signal(
            barrier, inc=1, device_id=partner, device_id_type=pl.DeviceIdType.MESH
        )

    rows = M // STEPS
    vec_in = [
        pltpu.make_async_copy(
            vec.at[pl.ds(i * rows, rows)], win.at[pl.ds(HALO + i * rows, rows)], vec_sem.at[i]
        )
        for i in range(STEPS)
    ]
    right_in = [
        [
            pltpu.make_async_copy(
                rights[l].at[pl.ds(i * rows, rows)],
                rt.at[pl.ds(i * rows, rows), pl.ds(l * RB, RB)],
                right_sem.at[i],
            )
            for l in range(2)
        ]
        for i in range(STEPS)
    ]
    near_in = pltpu.make_async_copy(near, nt.at[:, pl.ds(0, NNZ)], loc_sem.at[2])
    left_in = [
        pltpu.make_async_copy(
            lefts[l].at[pl.ds(c * ROWS, ROWS)], left.at[k, l, yh], loc_sem.at[l]
        )
        for l in range(2)
    ]
    for i in range(STEPS):
        for copy in right_in[i] + [vec_in[i]]:
            copy.start()

    pieces = [(s, core, l) for s in range(2) for core in range(2) for l in range(2)]
    hops = {}
    forwards = {}
    for s, core, l in pieces:
        for p in range(2):
            off = s * HALF + p * PIECE
            hops[p, s, core, l] = rcopy(
                lefts[l].at[pl.ds((oh * 2 + core) * ROWS + off, PIECE)],
                relay.at[p, s, core, l],
                hop_s.at[p, s],
                hop_r.at[p, s],
                dev(flip, highs[p], k),
            )
            forwards[p, s, core, l] = rcopy(
                relay.at[p, s, core, l],
                left.at[k, l, highs[p], pl.ds(off, PIECE)],
                fwd_s.at[p, s],
                fwd_r.at[s, k],
                dev(flip, highs[1 - p], core),
            )
    hop_all = {
        (p, s): rcopy(
            relay.at[p, s], relay.at[p, s], hop_s.at[p, s], hop_r.at[p, s], dev(flip, highs[p], k)
        )
        for p in range(2)
        for s in range(2)
    }
    fwd_all = {
        (p, s): rcopy(
            relay.at[p, s], relay.at[p, s], fwd_s.at[p, s], fwd_r.at[s, k], dev(flip, highs[p], k)
        )
        for p in range(2)
        for s in range(2)
    }

    def arrival(s, core):
        here = left.at[core, :, oh, pl.ds(s * HALF, HALF)]
        return rcopy(here, here, fwd_s.at[0, s], fwd_r.at[s, core], dev(flip, yh, k))

    swaps = [
        rcopy(
            lefts[l].at[pl.ds((yh * 2 + ok) * ROWS, ROWS)],
            left.at[k, l, yh],
            swap_s.at[l],
            swap_r.at[l],
            other,
        )
        for l in range(2)
    ]

    def hop_start(some):
        for s, core, l in some:
            for p in range(2):
                hops[p, s, core, l].start()

    def forward_start(s):
        for p in range(2):
            hop_all[p, s].wait_recv()
        for core in range(2):
            for l in range(2):
                for p in range(2):
                    forwards[p, s, core, l].start()

    def project(low, high):
        for i in range(low, high):
            taken = rt.at[pl.ds(i * rows, rows)]
            pltpu.make_async_copy(taken, taken, right_sem.at[i]).wait()
            vec_in[i].wait()
            term = lax.dot_general(
                rt[pl.ds(i * rows, rows), :],
                win[pl.ds(HALO + i * rows, rows), :],
                (((0,), (0,)), ((), ())),
                preferred_element_type=F32,
            )
            if i == 0:
                pacc[...] = term
            else:
                pacc[...] += term

    project(0, EARLY)
    pl.semaphore_wait(barrier, len(partners))
    hop_start(pieces[:FIRST])
    near_in.start()
    project(EARLY, STEPS)
    for l in range(2):
        for zz in range(4):
            part[zz, l] = pacc[pl.ds(l * RB + zz * 32, 32), :].astype(BF)
    ways = (dev(at_z(zp), yh, k), dev(at_z(zm), yh, k))
    nexts = (zp, zm)
    lasts = (zm, zp)
    halves = (pl.ds(0, 16), pl.ds(16, 16))
    z_hop = []
    z_out = []
    z_fwd = []
    for d in range(2):
        z_hop.append(
            rcopy(part.at[zo, :, halves[d]], zrelay.at[d], z_s.at[0, d], z_r.at[0, d], ways[d])
        )
        z_out.append(rcopy(part.at[nexts[d]], zin.at[z], z_s.at[1, d], z_r.at[1, d], ways[d]))
        z_fwd.append(
            rcopy(
                zrelay.at[d], zin.at[lasts[d], :, halves[d]], z_s.at[2, d], z_r.at[2, d], ways[d]
            )
        )
    for copy in z_hop + z_out:
        copy.start()

    near_base = pl.multiple_of((1 - yl) * (HALO + M), HALO)
    far_base = pl.multiple_of(yl * (HALO + M), HALO)
    edge = jnp.logical_and(r > 0, r < 31)
    relays = jnp.logical_and(flip > 0, flip < 31)
    far_out = rcopy(
        vec.at[pl.ds(yl * (M - HALO) + (2 * yh + k) * QUARTER, QUARTER)],
        far_rows,
        far_s.at[0],
        far_r.at[0],
        dev((r + 30 + 4 * yl) % 32, yh, k),
    )
    near_halo = []
    far_halo = []
    near_share = []
    far_share = []
    for p in range(2):
        quarter = (2 * p + k) * QUARTER
        for i in range(2):
            piece = quarter + i * (QUARTER // 2)
            near_halo.append(
                rcopy(
                    vec.at[pl.ds((1 - yl) * (M - HALO) + piece, QUARTER // 2)],
                    win.at[pl.ds(far_base + piece, QUARTER // 2)],
                    near_s.at[p, i],
                    near_r.at[p, i],
                    dev(flip, highs[p], k),
                )
            )
        place = win.at[pl.ds(near_base + quarter, QUARTER)]
        near_share.append(rcopy(place, place, share_s.at[0, p], share_r.at[0, p], other))
        far_halo.append(
            rcopy(
                far_rows,
                win.at[pl.ds(near_base + (2 * yh + k) * QUARTER, QUARTER)],
                halo_s.at[p],
                halo_r.at[p],
                dev(flip, highs[p], k),
            )
        )
        place = win.at[pl.ds(far_base + (2 * highs[p] + k) * QUARTER, QUARTER)]
        far_share.append(rcopy(place, place, share_s.at[1, p], share_r.at[1, p], other))

    for copy in swaps + left_in:
        copy.start()

    nt[:, NNZ] = jnp.zeros((TILES, B, B), BF)
    near_in.wait()
    for d in range(2):
        z_hop[d].wait_recv()
        z_fwd[d].start()

    @pl.when(edge)
    def _():
        far_out.start()

    def assemble(w, carry):
        for t in range(TILES):
            place = jnp.int32(NNZ)
            for j in range(NNZ):
                place = jnp.where(cols[t, j] == w, j, place)
            dense[pl.ds(t * B, B), pl.ds(pl.multiple_of(w * B, B), B)] = nt[t, place]
        return carry

    lax.fori_loop(0, WINDOW, assemble, 0)

    def near_part(first, depth, low, high, initial=False):
        def columns(i, carry):
            here = pl.ds(pl.multiple_of(i * B, B), B)
            term = jnp.dot(
                dense[:, pl.ds(first, depth)],
                win[pl.ds(first, depth), here],
                preferred_element_type=F32,
            )
            if initial:
                acc[:, here] = term
            else:
                acc[:, here] += term
            return carry

        lax.fori_loop(low, high, columns, 0)

    done = [0]

    def advance(count):
        while count > 0:
            slab, low = divmod(done[0], 4)
            high = min(4, low + count)
            near_part(HALO + slab * 1024, 1024, low, high, slab == 0)
            done[0] += high - low
            count -= high - low

    advance(PLAN[0])

    for copy in z_out + z_fwd:
        copy.wait_recv()
    for l in range(2):
        base = pl.multiple_of(l * RB + z * 32, 32)
        total = pacc[pl.ds(base, 32), :]
        for j in range(1, 4):
            total = total + zin[(z + j) % 4, l].astype(F32)
        pacc[pl.ds(base, 32), :] = total
        keep[l] = pacc[pl.ds(pl.multiple_of(base + yl * 16, 16), 16), :]
        ysend[l] = pacc[pl.ds(pl.multiple_of(base + (1 - yl) * 16, 16), 16), :].astype(BF)
    y_out = rcopy(ysend, yin, y_s.at[0], y_r.at[0], dev(flip, yh, k))
    y_out.start()
    hop_start(pieces[FIRST:])
    advance(PLAN[1])

    y_out.wait()
    for l in range(2):
        xsend[l] = (keep[l] + yin[l].astype(F32)).astype(BF)
    x_out = [
        rcopy(
            xsend.at[1], coeff.at[k, 1, yh, z, yl], x_s.at[0], x_r.at[0], dev(at_x(x1), yh, k)
        ),
        rcopy(xsend.at[0], xin.at[xpar], x_s.at[1], x_r.at[1], dev(at_x(x2), yh, k)),
        rcopy(xsend.at[0], xin.at[xpar], x_s.at[2], x_r.at[2], dev(at_x(x3), yh, k)),
    ]
    for i in (1, 2, 0):
        x_out[i].start()
    near_halo[0].start()
    near_halo[2].start()
    advance(PLAN[2])
    for copy in x_out:
        copy.wait_recv()
    coeff[k, 0, yh, z, yl] = (xin[0].astype(F32) + xin[1].astype(F32)).astype(BF)

    mine = coeff.at[k, :, yh, z, yl]
    g_out = [
        rcopy(mine, mine, g_s.at[i], g_r.at[i], target)
        for i, target in enumerate((dev(flip, yh, k), dev(flip, oh, k), dev(r, oh, k)))
    ]
    for i in (2, 0, 1):
        g_out[i].start()
    near_halo[1].start()
    near_halo[3].start()

    @pl.when(relays)
    def _():
        far_out.wait_recv()
        for copy in far_halo:
            copy.start()

    forward_start(0)
    advance(PLAN[3])
    for copy in g_out:
        copy.wait_recv()

    def level(l, zz):
        return coeff.at[k, l, :, zz]

    def ring_copy(l, zz, d, i):
        return rcopy(level(l, zz), level(l, zz), ring_s.at[d, i], ring_r.at[d, i], ways[d])

    ring = [
        [ring_copy(d, z, d, 0), ring_copy(1 - d, z, d, 1), ring_copy(d, lasts[d], d, 2)]
        for d in range(2)
    ]

    def core_start(l, zz):
        rcopy(level(l, zz), level(l, zz), core_s.at[0], core_r.at[0], other).start()

    core_out = rcopy(coeff.at[k], coeff.at[k], core_s.at[0], core_r.at[0], other)
    for i in range(2):
        for d in range(2):
            ring[d][i].start()
    for l in range(2):
        core_start(l, z)
    forward_start(1)
    advance(16 - done[0])
    for d in range(2):
        ring[d][0].wait_recv()
        ring[d][2].start()
        core_start(d, lasts[d])
    for copy in near_halo:
        copy.wait_recv()
    for copy in near_share:
        copy.start()
    for d in range(2):
        ring[d][1].wait_recv()
        core_start(1 - d, lasts[d])
    for copy in near_share:
        copy.wait_recv()
    near_part(near_base, HALO, 0, 4)

    @pl.when(edge)
    def _():
        for copy in far_halo:
            copy.wait_recv()
        for copy in far_share:
            copy.start()

    for d in range(2):
        ring[d][2].wait_recv()
        core_start(d, zo)

    @pl.when(edge)
    def _():
        for copy in far_share:
            copy.wait()

    @pl.when(jnp.logical_not(edge))
    def _():
        win[pl.ds(far_base, HALO), :] = jnp.zeros((HALO, N), BF)

    near_part(far_base, HALO, 0, 4)

    def far_part(chips, low, count, target):
        blocks = [(a, l, h) for a in range(2) for l in range(2) for h in chips]

        def columns(i, carry):
            here = pl.ds(pl.multiple_of(i * B, B), B)
            basis = jnp.concatenate([left[a, l, h, pl.ds(low, count)] for a, l, h in blocks], axis=1)
            weights = jnp.concatenate(
                [coeff[a, l, h, :, :, :, here].reshape(RB, B) for a, l, h in blocks], axis=0
            )
            term = jnp.dot(basis, weights, preferred_element_type=F32)
            total = acc[pl.ds(low, count), here] + term
            target[pl.ds(low, count), here] = total.astype(target.dtype)
            return carry

        lax.fori_loop(0, N // B, columns, 0)

    for copy in left_in:
        copy.wait()
    for copy in swaps:
        copy.wait_recv()
    core_out.wait_recv()
    far_part((yh,), HALF, HALF, acc)
    for core in range(2):
        arrival(0, core).wait_recv()
    far_part((0, 1), 0, HALF, out)
    for core in range(2):
        arrival(1, core).wait_recv()
    far_part((oh,), HALF, HALF, out)

    for copy in (
        list(hop_all.values())
        + list(fwd_all.values())
        + z_hop
        + z_out
        + z_fwd
        + x_out
        + g_out
        + ring[0]
        + ring[1]
        + [core_out]
        + swaps
        + near_halo
        + near_share
    ):
        copy.wait_send()

    @pl.when(edge)
    def _():
        far_out.wait_send()

    @pl.when(relays)
    def _():
        for copy in far_halo:
            copy.wait_send()


def per_device(vectors, near_tiles, near_cols, left_one, right_one, left_two, right_two):
    hbm = pl.BlockSpec(memory_space=pltpu.HBM)
    counts = [
        (STEPS,),
        (STEPS,),
        (3,),
        (2, 2),
        (2, 2),
        (2, 2),
        (2, 2),
        (2,),
        (2,),
        (1,),
        (1,),
        (2, 2),
        (2, 2),
        (2,),
        (2,),
        (2, 2),
        (2, 2),
        (3, 2),
        (3, 2),
        (1,),
        (1,),
        (3,),
        (3,),
        (3,),
        (3,),
        (2, 3),
        (2, 3),
        (1,),
        (1,),
    ]
    return pl.pallas_call(
        kernel,
        out_shape=pltpu.VMEM((ROWS, N), BF),
        in_specs=[pl.BlockSpec(memory_space=pltpu.SMEM)] + [hbm] * 6,
        out_specs=pl.BlockSpec(memory_space=pltpu.VMEM),
        scratch_shapes=[
            pltpu.VMEM((WINDOW * B, N), BF),
            pltpu.VMEM((TILES, NNZ + 1, B, B), BF),
            pltpu.VMEM((ROWS, WINDOW * B), BF),
            pltpu.VMEM((M, 2 * RB), BF),
            pltpu.VMEM((2 * RB, N), F32),
            pltpu.VMEM((4, 2, 32, N), BF),
            pltpu.VMEM((4, 2, 32, N), BF),
            pltpu.VMEM((2, 2, 16, N), BF),
            pltpu.VMEM((2, 16, N), BF),
            pltpu.VMEM((2, 16, N), BF),
            pltpu.VMEM((2, 16, N), F32),
            pltpu.VMEM((2, 16, N), BF),
            pltpu.VMEM((2, 16, N), BF),
            pltpu.VMEM((2, 2, 2, 4, 2, 16, N), BF),
            pltpu.VMEM((2, 2, 2, ROWS, RB), BF),
            pltpu.VMEM((2, 2, 2, 2, PIECE, RB), BF),
            pltpu.VMEM((QUARTER, N), BF),
            pltpu.VMEM((ROWS, N), F32),
        ]
        + [pltpu.SemaphoreType.DMA(shape) for shape in counts],
        compiler_params=pltpu.CompilerParams(
            collective_id=0, has_side_effects=True, vmem_limit_bytes=54 * 1024 * 1024
        ),
    )(near_cols, vectors, near_tiles, left_one, left_two, right_one, right_two)


def solution(mesh):
    placed = (
        P("rows", None),
        P(("rows", "cols"), None, None, None),
        P(("rows", "cols"), None),
        P("rows", "cols"),
        P("rows", "cols"),
        P("rows", "cols"),
        P("rows", "cols"),
    )
    return jax.shard_map(
        per_device, mesh=mesh, in_specs=placed, out_specs=P(("rows", "cols"), None), check_vma=False
    )
```

```python
import jax
import jax.numpy as jnp
from jax import lax
from jax.experimental import pallas as pl
from jax.experimental.pallas import tpu as pltpu
from jax.sharding import PartitionSpec as P

B = 256
REACH = 2
NNZ = 16
TILES = 4
OWN = 16
WINDOW = OWN + 2 * REACH
M = OWN * B
N = 1024
HALO = REACH * B
QUARTER = HALO // 4
ROWS = TILES * B
RB = 128
HALF = ROWS // 2
PIECE = HALF // 2
STEPS = 8
EARLY = 4
PLAN = (2, 6, 5)
BF = jnp.bfloat16
F32 = jnp.float32


def kernel(
    cols,
    vec,
    near,
    left_one,
    left_two,
    right_one,
    right_two,
    out,
    win,
    nt,
    dense,
    rt,
    pacc,
    part,
    zin,
    zrelay,
    xsend,
    xin,
    coeff,
    left,
    relay,
    far_rows,
    acc,
    vec_sem,
    right_sem,
    loc_sem,
    hop_s,
    hop_r,
    fwd_s,
    fwd_r,
    swap_s,
    swap_r,
    far_s,
    far_r,
    near_s,
    near_r,
    halo_s,
    halo_r,
    share_s,
    share_r,
    z_s,
    z_r,
    x_s,
    x_r,
    g_s,
    g_r,
    ring_s,
    ring_r,
    core_s,
    core_r,
):
    lefts = (left_one, left_two)
    rights = (right_one, right_two)
    r = lax.axis_index("rows")
    c = lax.axis_index("cols")
    x = r // 8
    z = (r // 2) % 4
    yl = r % 2
    yh = c // 2
    k = c % 2
    flip = r + 1 - 2 * yl
    oh = 1 - yh
    ok = 1 - k
    highs = (yh, oh)

    def dev(row, high, core):
        return (row, high * 2 + core)

    def at_z(zz):
        return x * 8 + zz * 2 + yl

    def at_x(xx):
        return xx * 8 + z * 2 + yl

    zp = (z + 1) % 4
    zm = (z + 3) % 4
    zo = (z + 2) % 4
    x1 = x + 1 - 2 * (x % 2)
    x2 = (x + 2) % 4
    x3 = 3 - x
    xpar = x % 2
    other = dev(r, yh, ok)

    def rcopy(src, dst, send, recv, target):
        return pltpu.make_async_remote_copy(
            src_ref=src,
            dst_ref=dst,
            send_sem=send,
            recv_sem=recv,
            device_id=target,
            device_id_type=pl.DeviceIdType.MESH,
        )

    barrier = pltpu.get_barrier_semaphore()
    partners = [
        dev(flip, yh, k),
        dev(flip, oh, k),
        dev(flip, yh, ok),
        dev(flip, oh, ok),
        dev(r, oh, k),
        other,
        dev(at_z(zp), yh, k),
        dev(at_z(zm), yh, k),
        dev(at_x(x1), yh, k),
        dev(at_x(x2), yh, k),
        dev(at_x(x3), yh, k),
        dev(at_x(x1) + flip - r, yh, k),
        dev(at_x(x2) + flip - r, yh, k),
        dev(at_x(x3) + flip - r, yh, k),
        dev((r + 2) % 32, yh, k),
        dev((r + 30) % 32, yh, k),
    ]
    for partner in partners:
        pl.semaphore_signal(
            barrier, inc=1, device_id=partner, device_id_type=pl.DeviceIdType.MESH
        )

    rows = M // STEPS
    vec_in = [
        pltpu.make_async_copy(
            vec.at[pl.ds(i * rows, rows)], win.at[pl.ds(HALO + i * rows, rows)], vec_sem.at[i]
        )
        for i in range(STEPS)
    ]
    right_in = [
        [
            pltpu.make_async_copy(
                rights[l].at[pl.ds(i * rows, rows)],
                rt.at[pl.ds(i * rows, rows), pl.ds(l * RB, RB)],
                right_sem.at[i],
            )
            for l in range(2)
        ]
        for i in range(STEPS)
    ]
    near_in = pltpu.make_async_copy(near, nt.at[:, pl.ds(0, NNZ)], loc_sem.at[2])
    left_in = [
        pltpu.make_async_copy(
            lefts[l].at[pl.ds(c * ROWS, ROWS)], left.at[k, l, yh], loc_sem.at[l]
        )
        for l in range(2)
    ]
    for i in range(STEPS):
        for copy in right_in[i] + [vec_in[i]]:
            copy.start()

    pieces = [(s, core, l) for s in range(2) for core in range(2) for l in range(2)]
    hops = {}
    forwards = {}
    for s, core, l in pieces:
        for p in range(2):
            off = s * HALF + p * PIECE
            hops[p, s, core, l] = rcopy(
                lefts[l].at[pl.ds((oh * 2 + core) * ROWS + off, PIECE)],
                relay.at[p, s, core, l],
                hop_s.at[p, s],
                hop_r.at[p, s],
                dev(flip, highs[p], k),
            )
            forwards[p, s, core, l] = rcopy(
                relay.at[p, s, core, l],
                left.at[k, l, highs[p], pl.ds(off, PIECE)],
                fwd_s.at[p, s],
                fwd_r.at[s, k],
                dev(flip, highs[1 - p], core),
            )
    hop_all = {
        (p, s): rcopy(
            relay.at[p, s], relay.at[p, s], hop_s.at[p, s], hop_r.at[p, s], dev(flip, highs[p], k)
        )
        for p in range(2)
        for s in range(2)
    }
    fwd_all = {
        (p, s): rcopy(
            relay.at[p, s], relay.at[p, s], fwd_s.at[p, s], fwd_r.at[s, k], dev(flip, highs[p], k)
        )
        for p in range(2)
        for s in range(2)
    }

    def arrival(s, core):
        here = left.at[core, :, oh, pl.ds(s * HALF, HALF)]
        return rcopy(here, here, fwd_s.at[0, s], fwd_r.at[s, core], dev(flip, yh, k))

    swaps = [
        rcopy(
            lefts[l].at[pl.ds((yh * 2 + ok) * ROWS, ROWS)],
            left.at[k, l, yh],
            swap_s.at[l],
            swap_r.at[l],
            other,
        )
        for l in range(2)
    ]

    def hop_start(some):
        for s, core, l in some:
            for p in range(2):
                hops[p, s, core, l].start()

    def forward_start(s):
        for p in range(2):
            hop_all[p, s].wait_recv()
        for core in range(2):
            for l in range(2):
                for p in range(2):
                    forwards[p, s, core, l].start()

    def project(low, high):
        for i in range(low, high):
            taken = rt.at[pl.ds(i * rows, rows)]
            pltpu.make_async_copy(taken, taken, right_sem.at[i]).wait()
            vec_in[i].wait()
            term = lax.dot_general(
                rt[pl.ds(i * rows, rows), :],
                win[pl.ds(HALO + i * rows, rows), :],
                (((0,), (0,)), ((), ())),
                preferred_element_type=F32,
            )
            if i == 0:
                pacc[...] = term
            else:
                pacc[...] += term

    project(0, EARLY)
    pl.semaphore_wait(barrier, len(partners))
    hop_start(pieces)
    near_in.start()
    project(EARLY, STEPS)
    for l in range(2):
        for zz in range(4):
            part[zz, l] = pacc[pl.ds(l * RB + zz * 32, 32), :].astype(BF)
    ways = (dev(at_z(zp), yh, k), dev(at_z(zm), yh, k))
    nexts = (zp, zm)
    lasts = (zm, zp)
    halves = (pl.ds(0, 16), pl.ds(16, 16))
    z_hop = []
    z_out = []
    z_fwd = []
    for d in range(2):
        z_hop.append(
            rcopy(part.at[zo, :, halves[d]], zrelay.at[d], z_s.at[0, d], z_r.at[0, d], ways[d])
        )
        z_out.append(rcopy(part.at[nexts[d]], zin.at[z], z_s.at[1, d], z_r.at[1, d], ways[d]))
        z_fwd.append(
            rcopy(
                zrelay.at[d], zin.at[lasts[d], :, halves[d]], z_s.at[2, d], z_r.at[2, d], ways[d]
            )
        )
    for copy in z_hop + z_out:
        copy.start()

    near_base = pl.multiple_of((1 - yl) * (HALO + M), HALO)
    far_base = pl.multiple_of(yl * (HALO + M), HALO)
    edge = jnp.logical_and(r > 0, r < 31)
    relays = jnp.logical_and(flip > 0, flip < 31)
    far_out = rcopy(
        vec.at[pl.ds(yl * (M - HALO) + (2 * yh + k) * QUARTER, QUARTER)],
        far_rows,
        far_s.at[0],
        far_r.at[0],
        dev((r + 30 + 4 * yl) % 32, yh, k),
    )
    near_halo = []
    far_halo = []
    near_share = []
    far_share = []
    for p in range(2):
        quarter = (2 * p + k) * QUARTER
        for i in range(2):
            piece = quarter + i * (QUARTER // 2)
            near_halo.append(
                rcopy(
                    vec.at[pl.ds((1 - yl) * (M - HALO) + piece, QUARTER // 2)],
                    win.at[pl.ds(far_base + piece, QUARTER // 2)],
                    near_s.at[p, i],
                    near_r.at[p, i],
                    dev(flip, highs[p], k),
                )
            )
        place = win.at[pl.ds(near_base + quarter, QUARTER)]
        near_share.append(rcopy(place, place, share_s.at[0, p], share_r.at[0, p], other))
        far_halo.append(
            rcopy(
                far_rows,
                win.at[pl.ds(near_base + (2 * yh + k) * QUARTER, QUARTER)],
                halo_s.at[p],
                halo_r.at[p],
                dev(flip, highs[p], k),
            )
        )
        place = win.at[pl.ds(far_base + (2 * highs[p] + k) * QUARTER, QUARTER)]
        far_share.append(rcopy(place, place, share_s.at[1, p], share_r.at[1, p], other))

    for copy in swaps + left_in:
        copy.start()

    nt[:, NNZ] = jnp.zeros((TILES, B, B), BF)
    near_in.wait()
    for d in range(2):
        z_hop[d].wait_recv()
        z_fwd[d].start()

    def assemble(w, carry):
        for t in range(TILES):
            place = jnp.int32(NNZ)
            for j in range(NNZ):
                place = jnp.where(cols[t, j] == w, j, place)
            dense[pl.ds(t * B, B), pl.ds(pl.multiple_of(w * B, B), B)] = nt[t, place]
        return carry

    lax.fori_loop(0, WINDOW, assemble, 0)

    def near_part(first, depth, low, high, initial=False):
        def columns(i, carry):
            here = pl.ds(pl.multiple_of(i * B, B), B)
            term = jnp.dot(
                dense[:, pl.ds(first, depth)],
                win[pl.ds(first, depth), here],
                preferred_element_type=F32,
            )
            if initial:
                acc[:, here] = term
            else:
                acc[:, here] += term
            return carry

        lax.fori_loop(low, high, columns, 0)

    done = [0]

    def advance(count):
        while count > 0:
            slab, low = divmod(done[0], 4)
            high = min(4, low + count)
            near_part(HALO + slab * 1024, 1024, low, high, slab == 0)
            done[0] += high - low
            count -= high - low

    advance(PLAN[0])

    for copy in z_out + z_fwd:
        copy.wait_recv()
    for l in range(2):
        base = pl.multiple_of(l * RB + z * 32, 32)
        total = pacc[pl.ds(base, 32), :]
        for j in range(1, 4):
            total = total + zin[(z + j) % 4, l].astype(F32)
        for low in range(2):
            xsend[l, low] = total[low * 16 : low * 16 + 16].astype(BF)

    for low in (1 - yl, yl):
        for l, plane, slot in ((0, x2, xpar), (0, x3, xpar), (1, x1, 2)):
            rcopy(
                xsend.at[l, low],
                xin.at[slot, yl],
                x_s.at[0],
                x_r.at[0],
                dev(plane * 8 + z * 2 + low, yh, k),
            ).start()
    x_all = rcopy(xin, xin, x_s.at[0], x_r.at[0], dev(at_x(x1), yh, k))
    for copy in near_halo:
        copy.start()

    @pl.when(edge)
    def _():
        far_out.start()

    advance(PLAN[1])
    x_all.wait_recv()
    first = xin[0, 0].astype(F32) + xin[0, 1].astype(F32)
    first = first + (xin[1, 0].astype(F32) + xin[1, 1].astype(F32))
    coeff[k, 0, yh, z, yl] = first.astype(BF)
    coeff[k, 1, yh, z, yl] = (xin[2, 0].astype(F32) + xin[2, 1].astype(F32)).astype(BF)

    mine = coeff.at[k, :, yh, z, yl]
    g_out = [
        rcopy(mine, mine, g_s.at[i], g_r.at[i], target)
        for i, target in enumerate((dev(flip, yh, k), dev(flip, oh, k), dev(r, oh, k)))
    ]
    for i in (2, 0, 1):
        g_out[i].start()

    @pl.when(relays)
    def _():
        far_out.wait_recv()
        for copy in far_halo:
            copy.start()

    forward_start(0)
    advance(PLAN[2])
    for copy in g_out:
        copy.wait_recv()

    def level(l, zz):
        return coeff.at[k, l, :, zz]

    def ring_copy(l, zz, d, i):
        return rcopy(level(l, zz), level(l, zz), ring_s.at[d, i], ring_r.at[d, i], ways[d])

    ring = [
        [ring_copy(d, z, d, 0), ring_copy(1 - d, z, d, 1), ring_copy(d, lasts[d], d, 2)]
        for d in range(2)
    ]

    def core_start(l, zz):
        rcopy(level(l, zz), level(l, zz), core_s.at[0], core_r.at[0], other).start()

    core_out = rcopy(coeff.at[k], coeff.at[k], core_s.at[0], core_r.at[0], other)
    for i in range(2):
        for d in range(2):
            ring[d][i].start()
    for l in range(2):
        core_start(l, z)
    forward_start(1)
    advance(16 - done[0])
    for copy in near_halo:
        copy.wait_recv()
    for copy in near_share:
        copy.start()
    for d in range(2):
        ring[d][0].wait_recv()
        ring[d][2].start()
        core_start(d, lasts[d])
    for copy in near_share:
        copy.wait_recv()
    near_part(near_base, HALO, 0, 4)
    for d in range(2):
        ring[d][1].wait_recv()
        core_start(1 - d, lasts[d])

    @pl.when(edge)
    def _():
        for copy in far_halo:
            copy.wait_recv()
        for copy in far_share:
            copy.start()

    for d in range(2):
        ring[d][2].wait_recv()
        core_start(d, zo)

    @pl.when(edge)
    def _():
        for copy in far_share:
            copy.wait()

    @pl.when(jnp.logical_not(edge))
    def _():
        win[pl.ds(far_base, HALO), :] = jnp.zeros((HALO, N), BF)

    near_part(far_base, HALO, 0, 4)

    def far_part(chips, low, count, target):
        blocks = [(a, l, h) for a in range(2) for l in range(2) for h in chips]

        def columns(i, carry):
            here = pl.ds(pl.multiple_of(i * B, B), B)
            basis = jnp.concatenate([left[a, l, h, pl.ds(low, count)] for a, l, h in blocks], axis=1)
            weights = jnp.concatenate(
                [coeff[a, l, h, :, :, :, here].reshape(RB, B) for a, l, h in blocks], axis=0
            )
            term = jnp.dot(basis, weights, preferred_element_type=F32)
            total = acc[pl.ds(low, count), here] + term
            target[pl.ds(low, count), here] = total.astype(target.dtype)
            return carry

        lax.fori_loop(0, N // B, columns, 0)

    for copy in left_in:
        copy.wait()
    for copy in swaps:
        copy.wait_recv()
    core_out.wait_recv()
    far_part((yh,), HALF, HALF, acc)
    for core in range(2):
        arrival(0, core).wait_recv()
    far_part((0, 1), 0, HALF, out)
    for core in range(2):
        arrival(1, core).wait_recv()
    far_part((oh,), HALF, HALF, out)

    for copy in (
        list(hop_all.values())
        + list(fwd_all.values())
        + z_hop
        + z_out
        + z_fwd
        + [x_all]
        + g_out
        + ring[0]
        + ring[1]
        + [core_out]
        + swaps
        + near_halo
        + near_share
    ):
        copy.wait_send()

    @pl.when(edge)
    def _():
        far_out.wait_send()

    @pl.when(relays)
    def _():
        for copy in far_halo:
            copy.wait_send()


def per_device(vectors, near_tiles, near_cols, left_one, right_one, left_two, right_two):
    hbm = pl.BlockSpec(memory_space=pltpu.HBM)
    counts = [
        (STEPS,),
        (STEPS,),
        (3,),
        (2, 2),
        (2, 2),
        (2, 2),
        (2, 2),
        (2,),
        (2,),
        (1,),
        (1,),
        (2, 2),
        (2, 2),
        (2,),
        (2,),
        (2, 2),
        (2, 2),
        (3, 2),
        (3, 2),
        (1,),
        (1,),
        (3,),
        (3,),
        (2, 3),
        (2, 3),
        (1,),
        (1,),
    ]
    return pl.pallas_call(
        kernel,
        out_shape=pltpu.VMEM((ROWS, N), BF),
        in_specs=[pl.BlockSpec(memory_space=pltpu.SMEM)] + [hbm] * 6,
        out_specs=pl.BlockSpec(memory_space=pltpu.VMEM),
        scratch_shapes=[
            pltpu.VMEM((WINDOW * B, N), BF),
            pltpu.VMEM((TILES, NNZ + 1, B, B), BF),
            pltpu.VMEM((ROWS, WINDOW * B), BF),
            pltpu.VMEM((M, 2 * RB), BF),
            pltpu.VMEM((2 * RB, N), F32),
            pltpu.VMEM((4, 2, 32, N), BF),
            pltpu.VMEM((4, 2, 32, N), BF),
            pltpu.VMEM((2, 2, 16, N), BF),
            pltpu.VMEM((2, 2, 16, N), BF),
            pltpu.VMEM((3, 2, 16, N), BF),
            pltpu.VMEM((2, 2, 2, 4, 2, 16, N), BF),
            pltpu.VMEM((2, 2, 2, ROWS, RB), BF),
            pltpu.VMEM((2, 2, 2, 2, PIECE, RB), BF),
            pltpu.VMEM((QUARTER, N), BF),
            pltpu.VMEM((ROWS, N), F32),
        ]
        + [pltpu.SemaphoreType.DMA(shape) for shape in counts],
        compiler_params=pltpu.CompilerParams(
            collective_id=0, has_side_effects=True, vmem_limit_bytes=54 * 1024 * 1024
        ),
    )(near_cols, vectors, near_tiles, left_one, left_two, right_one, right_two)


def solution(mesh):
    placed = (
        P("rows", None),
        P(("rows", "cols"), None, None, None),
        P(("rows", "cols"), None),
        P("rows", "cols"),
        P("rows", "cols"),
        P("rows", "cols"),
        P("rows", "cols"),
    )
    return jax.shard_map(
        per_device, mesh=mesh, in_specs=placed, out_specs=P(("rows", "cols"), None), check_vma=False
    )
```

```python
import jax
import jax.numpy as jnp
from jax import lax
from jax.experimental import pallas as pl
from jax.experimental.pallas import tpu as pltpu
from jax.sharding import PartitionSpec as P

B = 256
REACH = 2
NNZ = 16
TILES = 4
OWN = 16
WINDOW = OWN + 2 * REACH
M = OWN * B
N = 1024
HALO = REACH * B
QUARTER = HALO // 4
ROWS = TILES * B
RB = 128
HALF = ROWS // 2
BLOCKS = ((0, 768), (768, 256))
SPLIT = ((80, 32), (112, 32))
STEPS = 8
EARLY = 1
PLAN = (5, 5, 3)
BF = jnp.bfloat16
F32 = jnp.float32


def kernel(
    cols,
    vec,
    near,
    left_one,
    left_two,
    right_one,
    right_two,
    out,
    win,
    nt,
    dense,
    rt,
    pacc,
    part,
    zin,
    zrelay,
    xsend,
    xin,
    coeff,
    left,
    relay,
    far_rows,
    acc,
    vec_sem,
    right_sem,
    loc_sem,
    hop_s,
    hop_r,
    fwd_s,
    fwd_r,
    swap_s,
    swap_r,
    far_s,
    far_r,
    near_s,
    near_r,
    halo_s,
    halo_r,
    share_s,
    share_r,
    z_s,
    z_r,
    x_s,
    x_r,
    g_s,
    g_r,
    ring_s,
    ring_r,
    core_s,
    core_r,
):
    lefts = (left_one, left_two)
    rights = (right_one, right_two)
    r = lax.axis_index("rows")
    c = lax.axis_index("cols")
    x = r // 8
    z = (r // 2) % 4
    yl = r % 2
    yh = c // 2
    k = c % 2
    flip = r + 1 - 2 * yl
    oh = 1 - yh
    ok = 1 - k
    highs = (yh, oh)

    def dev(row, high, core):
        return (row, high * 2 + core)

    def at_z(zz):
        return x * 8 + zz * 2 + yl

    def at_x(xx):
        return xx * 8 + z * 2 + yl

    zp = (z + 1) % 4
    zm = (z + 3) % 4
    zo = (z + 2) % 4
    x1 = x + 1 - 2 * (x % 2)
    x2 = (x + 2) % 4
    x3 = 3 - x
    xpar = x % 2
    other = dev(r, yh, ok)

    def rcopy(src, dst, send, recv, target):
        return pltpu.make_async_remote_copy(
            src_ref=src,
            dst_ref=dst,
            send_sem=send,
            recv_sem=recv,
            device_id=target,
            device_id_type=pl.DeviceIdType.MESH,
        )

    barrier = pltpu.get_barrier_semaphore()
    partners = [
        dev(flip, yh, k),
        dev(flip, oh, k),
        dev(flip, yh, ok),
        dev(flip, oh, ok),
        other,
        dev(at_z(zp), yh, k),
        dev(at_z(zm), yh, k),
        dev(at_x(x1), yh, k),
        dev(at_x(x2), yh, k),
        dev(at_x(x3), yh, k),
        dev(at_x(x1) + flip - r, yh, k),
        dev(at_x(x2) + flip - r, yh, k),
        dev(at_x(x3) + flip - r, yh, k),
        dev((r + 2) % 32, yh, k),
        dev((r + 30) % 32, yh, k),
    ]
    for partner in partners:
        pl.semaphore_signal(
            barrier, inc=1, device_id=partner, device_id_type=pl.DeviceIdType.MESH
        )

    rows = M // STEPS
    vec_in = [
        pltpu.make_async_copy(
            vec.at[pl.ds(i * rows, rows)], win.at[pl.ds(HALO + i * rows, rows)], vec_sem.at[i]
        )
        for i in range(STEPS)
    ]
    right_in = [
        [
            pltpu.make_async_copy(
                rights[l].at[pl.ds(i * rows, rows)],
                rt.at[pl.ds(i * rows, rows), pl.ds(l * RB, RB)],
                right_sem.at[i],
            )
            for l in range(2)
        ]
        for i in range(STEPS)
    ]
    near_in = pltpu.make_async_copy(near, nt.at[:, pl.ds(0, NNZ)], loc_sem.at[2])
    left_in = [
        pltpu.make_async_copy(
            lefts[l].at[pl.ds(c * ROWS, ROWS)], left.at[k, l, yh], loc_sem.at[l]
        )
        for l in range(2)
    ]
    for i in range(STEPS):
        for copy in right_in[i] + [vec_in[i]]:
            copy.start()

    pieces = [(s, core, l) for s in range(2) for core in range(2) for l in range(2)]
    hops = {}
    forwards = {}
    def slot(p, s, core=slice(None), l=slice(None)):
        return relay.at[p, core, l, pl.ds(BLOCKS[s][0] // 2, BLOCKS[s][1] // 2)]

    def part_of(p, s):
        return BLOCKS[s][0] + p * (BLOCKS[s][1] // 2), BLOCKS[s][1] // 2

    for s, core, l in pieces:
        for p in range(2):
            off, size = part_of(p, s)
            hops[p, s, core, l] = rcopy(
                lefts[l].at[pl.ds((oh * 2 + core) * ROWS + off, size)],
                slot(p, s, core, l),
                hop_s.at[p, s],
                hop_r.at[p, s],
                dev(flip, highs[p], k),
            )
            forwards[p, s, core, l] = rcopy(
                slot(p, s, core, l),
                left.at[k, l, highs[p], pl.ds(off, size)],
                fwd_s.at[p, s],
                fwd_r.at[s, k],
                dev(flip, highs[1 - p], core),
            )
    hop_all = {
        (p, s): rcopy(
            slot(p, s), slot(p, s), hop_s.at[p, s], hop_r.at[p, s], dev(flip, highs[p], k)
        )
        for p in range(2)
        for s in range(2)
    }
    fwd_all = {
        (p, s): rcopy(
            slot(p, s), slot(p, s), fwd_s.at[p, s], fwd_r.at[s, k], dev(flip, highs[p], k)
        )
        for p in range(2)
        for s in range(2)
    }

    def arrival(s, core):
        here = left.at[core, :, oh, pl.ds(*BLOCKS[s])]
        return rcopy(here, here, fwd_s.at[0, s], fwd_r.at[s, core], dev(flip, yh, k))

    swaps = [
        rcopy(
            lefts[l].at[pl.ds((yh * 2 + ok) * ROWS, ROWS)],
            left.at[k, l, yh],
            swap_s.at[l],
            swap_r.at[l],
            other,
        )
        for l in range(2)
    ]

    def hop_start(some):
        for s, core, l in some:
            for p in range(2):
                hops[p, s, core, l].start()

    def forward_start(s):
        for p in range(2):
            hop_all[p, s].wait_recv()
        for core in range(2):
            for l in range(2):
                for p in range(2):
                    forwards[p, s, core, l].start()

    def project(low, high):
        for i in range(low, high):
            taken = rt.at[pl.ds(i * rows, rows)]
            pltpu.make_async_copy(taken, taken, right_sem.at[i]).wait()
            vec_in[i].wait()
            term = lax.dot_general(
                rt[pl.ds(i * rows, rows), :],
                win[pl.ds(HALO + i * rows, rows), :],
                (((0,), (0,)), ((), ())),
                preferred_element_type=F32,
            )
            if i == 0:
                pacc[...] = term
            else:
                pacc[...] += term

    project(0, EARLY)
    pl.semaphore_wait(barrier, len(partners))
    hop_start(pieces)
    near_in.start()
    project(EARLY, STEPS)
    for l in range(2):
        for zz in range(4):
            part[zz, l] = pacc[pl.ds(l * RB + zz * 32, 32), :].astype(BF)
    ways = (dev(at_z(zp), yh, k), dev(at_z(zm), yh, k))
    nexts = (zp, zm)
    lasts = (zm, zp)
    halves = (pl.ds(0, 16), pl.ds(16, 16))
    z_hop = []
    z_out = []
    z_fwd = []
    for d in range(2):
        z_hop.append(
            rcopy(part.at[zo, :, halves[d]], zrelay.at[d], z_s.at[0, d], z_r.at[0, d], ways[d])
        )
        z_out.append(rcopy(part.at[nexts[d]], zin.at[z], z_s.at[1, d], z_r.at[1, d], ways[d]))
        z_fwd.append(
            rcopy(
                zrelay.at[d], zin.at[lasts[d], :, halves[d]], z_s.at[2, d], z_r.at[2, d], ways[d]
            )
        )
    for copy in z_hop + z_out:
        copy.start()

    near_base = pl.multiple_of((1 - yl) * (HALO + M), HALO)
    far_base = pl.multiple_of(yl * (HALO + M), HALO)
    edge = jnp.logical_and(r > 0, r < 31)
    relays = jnp.logical_and(flip > 0, flip < 31)
    far_out = rcopy(
        vec.at[pl.ds(yl * (M - HALO) + (2 * yh + k) * QUARTER, QUARTER)],
        far_rows,
        far_s.at[0],
        far_r.at[0],
        dev((r + 30 + 4 * yl) % 32, yh, k),
    )
    near_halo = []
    far_halo = []
    near_share = []
    far_share = []
    for p in range(2):
        half = k * (HALO // 2) + p * sum(SPLIT[0])
        for i in range(2):
            mine = half + i * SPLIT[p][0]
            near_halo.append(
                rcopy(
                    vec.at[pl.ds((1 - yl) * (M - HALO) + mine, SPLIT[p][i])],
                    win.at[pl.ds(far_base + mine, SPLIT[p][i])],
                    near_s.at[p, i],
                    near_r.at[p, i],
                    dev(flip, highs[p], k),
                )
            )
        place = win.at[pl.ds(near_base + half, sum(SPLIT[p]))]
        near_share.append(rcopy(place, place, share_s.at[0, p], share_r.at[0, p], other))
        far_halo.append(
            rcopy(
                far_rows,
                win.at[pl.ds(near_base + (2 * yh + k) * QUARTER, QUARTER)],
                halo_s.at[p],
                halo_r.at[p],
                dev(flip, highs[p], k),
            )
        )
        place = win.at[pl.ds(far_base + (2 * highs[p] + k) * QUARTER, QUARTER)]
        far_share.append(rcopy(place, place, share_s.at[1, p], share_r.at[1, p], other))

    for copy in swaps + left_in:
        copy.start()

    nt[:, NNZ] = jnp.zeros((TILES, B, B), BF)
    near_in.wait()

    def assemble(w, carry):
        for t in range(TILES):
            place = jnp.int32(NNZ)
            for j in range(NNZ):
                place = jnp.where(cols[t, j] == w, j, place)
            dense[pl.ds(t * B, B), pl.ds(pl.multiple_of(w * B, B), B)] = nt[t, place]
        return carry

    lax.fori_loop(0, WINDOW, assemble, 0)
    for d in range(2):
        z_hop[d].wait_recv()
        z_fwd[d].start()

    def near_part(first, depth, low, high, initial=False):
        def columns(i, carry):
            here = pl.ds(pl.multiple_of(i * B, B), B)
            term = jnp.dot(
                dense[:, pl.ds(first, depth)],
                win[pl.ds(first, depth), here],
                preferred_element_type=F32,
            )
            if initial:
                acc[:, here] = term
            else:
                acc[:, here] += term
            return carry

        lax.fori_loop(low, high, columns, 0)

    done = [0]

    def advance(count):
        while count > 0:
            slab, low = divmod(done[0], 4)
            high = min(4, low + count)
            near_part(HALO + slab * 1024, 1024, low, high, slab == 0)
            done[0] += high - low
            count -= high - low

    advance(PLAN[0])

    for copy in z_out + z_fwd:
        copy.wait_recv()
    for l in range(2):
        base = pl.multiple_of(l * RB + z * 32, 32)
        total = pacc[pl.ds(base, 32), :]
        for j in range(1, 4):
            total = total + zin[(z + j) % 4, l].astype(F32)
        for low in range(2):
            xsend[l, low] = total[low * 16 : low * 16 + 16].astype(BF)

    for low in (1 - yl, yl):
        for l, plane, place in ((0, x2, xpar), (0, x3, xpar), (1, x1, 2)):
            rcopy(
                xsend.at[l, low],
                xin.at[place, yl],
                x_s.at[0],
                x_r.at[0],
                dev(plane * 8 + z * 2 + low, yh, k),
            ).start()
    x_all = rcopy(xin, xin, x_s.at[0], x_r.at[0], dev(at_x(x1), yh, k))
    for p in range(2):
        near_halo[2 * p].start()

    @pl.when(edge)
    def _():
        far_out.start()

    advance(PLAN[1])
    x_all.wait_recv()
    first = xin[0, 0].astype(F32) + xin[0, 1].astype(F32)
    first = first + (xin[1, 0].astype(F32) + xin[1, 1].astype(F32))
    coeff[k, 0, yh, z, yl] = first.astype(BF)
    coeff[k, 1, yh, z, yl] = (xin[2, 0].astype(F32) + xin[2, 1].astype(F32)).astype(BF)

    mine = coeff.at[k, :, yh, z, yl]
    g_out = [
        rcopy(mine, mine, g_s.at[p], g_r.at[p], dev(flip, highs[p], k)) for p in range(2)
    ]
    g_fwd = []
    for l in range(2):
        theirs = coeff.at[k, l, highs[l], z, 1 - yl]
        g_fwd.append(
            rcopy(theirs, theirs, g_s.at[2 + l], g_r.at[2 + l], dev(flip, highs[1 - l], k))
        )
    for copy in g_out:
        copy.start()
    for p in range(2):
        near_halo[2 * p + 1].start()
    advance(PLAN[2])
    for p in range(2):
        g_out[p].wait_recv()
        g_fwd[p].start()

    @pl.when(relays)
    def _():
        far_out.wait_recv()
        for copy in far_halo:
            copy.start()

    forward_start(0)
    advance(16 - done[0])
    for copy in g_fwd:
        copy.wait_recv()

    def level(l, zz):
        return coeff.at[k, l, :, zz]

    def ring_copy(l, zz, d, i):
        return rcopy(level(l, zz), level(l, zz), ring_s.at[d, i], ring_r.at[d, i], ways[d])

    ring = [
        [ring_copy(d, z, d, 0), ring_copy(1 - d, z, d, 1), ring_copy(d, lasts[d], d, 2)]
        for d in range(2)
    ]

    def core_start(l, zz):
        rcopy(level(l, zz), level(l, zz), core_s.at[0], core_r.at[0], other).start()

    core_out = rcopy(coeff.at[k], coeff.at[k], core_s.at[0], core_r.at[0], other)
    for i in range(2):
        for d in range(2):
            ring[d][i].start()
    for l in range(2):
        core_start(l, z)
    forward_start(1)
    for copy in near_halo:
        copy.wait_recv()
    for copy in near_share:
        copy.start()
    for d in range(2):
        ring[d][0].wait_recv()
        ring[d][2].start()
        core_start(d, lasts[d])

    @pl.when(edge)
    def _():
        for copy in far_halo:
            copy.wait_recv()
        for copy in far_share:
            copy.start()

    for copy in near_share:
        copy.wait_recv()
    near_part(near_base, HALO, 0, 4)
    for d in range(2):
        ring[d][1].wait_recv()
        core_start(1 - d, lasts[d])

    for d in range(2):
        ring[d][2].wait_recv()
        core_start(d, zo)

    def far_part(chips, low, count, target):
        blocks = [(a, l, h) for a in range(2) for l in range(2) for h in chips]

        def columns(i, carry):
            here = pl.ds(pl.multiple_of(i * B, B), B)
            basis = jnp.concatenate([left[a, l, h, pl.ds(low, count)] for a, l, h in blocks], axis=1)
            weights = jnp.concatenate(
                [coeff[a, l, h, :, :, :, here].reshape(RB, B) for a, l, h in blocks], axis=0
            )
            term = jnp.dot(basis, weights, preferred_element_type=F32)
            total = acc[pl.ds(low, count), here] + term
            target[pl.ds(low, count), here] = total.astype(target.dtype)
            return carry

        lax.fori_loop(0, N // B, columns, 0)

    for copy in left_in:
        copy.wait()
    for copy in swaps:
        copy.wait_recv()
    core_out.wait_recv()
    far_part((yh,), 0, ROWS, acc)

    @pl.when(edge)
    def _():
        for copy in far_share:
            copy.wait()

    @pl.when(jnp.logical_not(edge))
    def _():
        win[pl.ds(far_base, HALO), :] = jnp.zeros((HALO, N), BF)

    near_part(far_base, HALO, 0, 4)
    for core in range(2):
        arrival(0, core).wait_recv()
    far_part((oh,), *BLOCKS[0], out)
    for core in range(2):
        arrival(1, core).wait_recv()
    far_part((oh,), *BLOCKS[1], out)

    for copy in (
        list(hop_all.values())
        + list(fwd_all.values())
        + z_hop
        + z_out
        + z_fwd
        + [x_all]
        + g_out
        + g_fwd
        + ring[0]
        + ring[1]
        + [core_out]
        + swaps
        + near_halo
        + near_share
    ):
        copy.wait_send()

    @pl.when(edge)
    def _():
        far_out.wait_send()

    @pl.when(relays)
    def _():
        for copy in far_halo:
            copy.wait_send()


def per_device(vectors, near_tiles, near_cols, left_one, right_one, left_two, right_two):
    hbm = pl.BlockSpec(memory_space=pltpu.HBM)
    counts = [
        (STEPS,),
        (STEPS,),
        (3,),
        (2, 2),
        (2, 2),
        (2, 2),
        (2, 2),
        (2,),
        (2,),
        (1,),
        (1,),
        (2, 2),
        (2, 2),
        (2,),
        (2,),
        (2, 2),
        (2, 2),
        (3, 2),
        (3, 2),
        (1,),
        (1,),
        (4,),
        (4,),
        (2, 3),
        (2, 3),
        (1,),
        (1,),
    ]
    return pl.pallas_call(
        kernel,
        out_shape=pltpu.VMEM((ROWS, N), BF),
        in_specs=[pl.BlockSpec(memory_space=pltpu.SMEM)] + [hbm] * 6,
        out_specs=pl.BlockSpec(memory_space=pltpu.VMEM),
        scratch_shapes=[
            pltpu.VMEM((WINDOW * B, N), BF),
            pltpu.VMEM((TILES, NNZ + 1, B, B), BF),
            pltpu.VMEM((ROWS, WINDOW * B), BF),
            pltpu.VMEM((M, 2 * RB), BF),
            pltpu.VMEM((2 * RB, N), F32),
            pltpu.VMEM((4, 2, 32, N), BF),
            pltpu.VMEM((4, 2, 32, N), BF),
            pltpu.VMEM((2, 2, 16, N), BF),
            pltpu.VMEM((2, 2, 16, N), BF),
            pltpu.VMEM((3, 2, 16, N), BF),
            pltpu.VMEM((2, 2, 2, 4, 2, 16, N), BF),
            pltpu.VMEM((2, 2, 2, ROWS, RB), BF),
            pltpu.VMEM((2, 2, 2, HALF, RB), BF),
            pltpu.VMEM((QUARTER, N), BF),
            pltpu.VMEM((ROWS, N), F32),
        ]
        + [pltpu.SemaphoreType.DMA(shape) for shape in counts],
        compiler_params=pltpu.CompilerParams(
            collective_id=0, has_side_effects=True, vmem_limit_bytes=54 * 1024 * 1024
        ),
    )(near_cols, vectors, near_tiles, left_one, left_two, right_one, right_two)


def solution(mesh):
    placed = (
        P("rows", None),
        P(("rows", "cols"), None, None, None),
        P(("rows", "cols"), None),
        P("rows", "cols"),
        P("rows", "cols"),
        P("rows", "cols"),
        P("rows", "cols"),
    )
    return jax.shard_map(
        per_device, mesh=mesh, in_specs=placed, out_specs=P(("rows", "cols"), None), check_vma=False
    )
```

```python
import jax
import jax.numpy as jnp
from jax import lax
from jax.experimental import pallas as pl
from jax.experimental.pallas import tpu as pltpu
from jax.sharding import PartitionSpec as P

B = 256
REACH = 2
NNZ = 16
TILES = 4
OWN = 16
WINDOW = OWN + 2 * REACH
M = OWN * B
N = 1024
HALO = REACH * B
QUARTER = HALO // 4
ROWS = TILES * B
RB = 128
HALF = ROWS // 2
BLOCKS = ((0, 768), (768, 256))
SPLIT = ((48, 64), (80, 64))
STEPS = 8
EARLY = 2
PLAN = (5, 5, 5)
BF = jnp.bfloat16
F32 = jnp.float32


def kernel(
    cols,
    vec,
    near,
    left_one,
    left_two,
    right_one,
    right_two,
    out,
    win,
    nt,
    dense,
    rt,
    pacc,
    part,
    zin,
    zrelay,
    xsend,
    xin,
    coeff,
    left,
    relay,
    far_rows,
    acc,
    vec_sem,
    right_sem,
    loc_sem,
    hop_s,
    hop_r,
    fwd_s,
    fwd_r,
    swap_s,
    swap_r,
    far_s,
    far_r,
    near_s,
    near_r,
    halo_s,
    halo_r,
    share_s,
    share_r,
    z_s,
    z_r,
    x_s,
    x_r,
    g_s,
    g_r,
    ring_s,
    ring_r,
    core_s,
    core_r,
):
    lefts = (left_one, left_two)
    rights = (right_one, right_two)
    r = lax.axis_index("rows")
    c = lax.axis_index("cols")
    x = r // 8
    z = (r // 2) % 4
    yl = r % 2
    yh = c // 2
    k = c % 2
    flip = r + 1 - 2 * yl
    oh = 1 - yh
    ok = 1 - k
    highs = (yh, oh)

    def dev(row, high, core):
        return (row, high * 2 + core)

    def at_z(zz):
        return x * 8 + zz * 2 + yl

    def at_x(xx):
        return xx * 8 + z * 2 + yl

    zp = (z + 1) % 4
    zm = (z + 3) % 4
    zo = (z + 2) % 4
    x1 = x + 1 - 2 * (x % 2)
    x2 = (x + 2) % 4
    x3 = 3 - x
    xpar = x % 2
    other = dev(r, yh, ok)

    def rcopy(src, dst, send, recv, target):
        return pltpu.make_async_remote_copy(
            src_ref=src,
            dst_ref=dst,
            send_sem=send,
            recv_sem=recv,
            device_id=target,
            device_id_type=pl.DeviceIdType.MESH,
        )

    barrier = pltpu.get_barrier_semaphore()
    partners = [
        dev(flip, yh, k),
        dev(flip, oh, k),
        dev(flip, yh, ok),
        dev(flip, oh, ok),
        dev(r, oh, k),
        other,
        dev(at_z(zp), yh, k),
        dev(at_z(zm), yh, k),
        dev(at_x(x1), yh, k),
        dev(at_x(x2), yh, k),
        dev(at_x(x3), yh, k),
        dev(at_x(x1) + flip - r, yh, k),
        dev(at_x(x2) + flip - r, yh, k),
        dev(at_x(x3) + flip - r, yh, k),
        dev((r + 2) % 32, yh, k),
        dev((r + 30) % 32, yh, k),
    ]
    for partner in partners:
        pl.semaphore_signal(
            barrier, inc=1, device_id=partner, device_id_type=pl.DeviceIdType.MESH
        )

    rows = M // STEPS
    vec_in = [
        pltpu.make_async_copy(
            vec.at[pl.ds(i * rows, rows)], win.at[pl.ds(HALO + i * rows, rows)], vec_sem.at[i]
        )
        for i in range(STEPS)
    ]
    right_in = [
        [
            pltpu.make_async_copy(
                rights[l].at[pl.ds(i * rows, rows)],
                rt.at[pl.ds(i * rows, rows), pl.ds(l * RB, RB)],
                right_sem.at[i],
            )
            for l in range(2)
        ]
        for i in range(STEPS)
    ]
    near_in = pltpu.make_async_copy(near, nt.at[:, pl.ds(0, NNZ)], loc_sem.at[2])
    left_in = [
        pltpu.make_async_copy(
            lefts[l].at[pl.ds(c * ROWS, ROWS)], left.at[k, l, yh], loc_sem.at[l]
        )
        for l in range(2)
    ]
    for i in range(STEPS):
        for copy in right_in[i] + [vec_in[i]]:
            copy.start()

    pieces = [(s, core, l) for s in range(2) for core in range(2) for l in range(2)]
    hops = {}
    forwards = {}
    def slot(p, s, core=slice(None), l=slice(None)):
        return relay.at[p, core, l, pl.ds(BLOCKS[s][0] // 2, BLOCKS[s][1] // 2)]

    def part_of(p, s):
        return BLOCKS[s][0] + p * (BLOCKS[s][1] // 2), BLOCKS[s][1] // 2

    for s, core, l in pieces:
        for p in range(2):
            off, size = part_of(p, s)
            hops[p, s, core, l] = rcopy(
                lefts[l].at[pl.ds((oh * 2 + core) * ROWS + off, size)],
                slot(p, s, core, l),
                hop_s.at[p, s],
                hop_r.at[p, s],
                dev(flip, highs[p], k),
            )
            forwards[p, s, core, l] = rcopy(
                slot(p, s, core, l),
                left.at[k, l, highs[p], pl.ds(off, size)],
                fwd_s.at[p, s],
                fwd_r.at[s, k],
                dev(flip, highs[1 - p], core),
            )
    hop_all = {
        (p, s): rcopy(
            slot(p, s), slot(p, s), hop_s.at[p, s], hop_r.at[p, s], dev(flip, highs[p], k)
        )
        for p in range(2)
        for s in range(2)
    }
    fwd_all = {
        (p, s): rcopy(
            slot(p, s), slot(p, s), fwd_s.at[p, s], fwd_r.at[s, k], dev(flip, highs[p], k)
        )
        for p in range(2)
        for s in range(2)
    }

    def arrival(s, core):
        here = left.at[core, :, oh, pl.ds(*BLOCKS[s])]
        return rcopy(here, here, fwd_s.at[0, s], fwd_r.at[s, core], dev(flip, yh, k))

    swaps = [
        rcopy(
            lefts[l].at[pl.ds((yh * 2 + ok) * ROWS, ROWS)],
            left.at[k, l, yh],
            swap_s.at[l],
            swap_r.at[l],
            other,
        )
        for l in range(2)
    ]

    def hop_start(some):
        for s, core, l in some:
            for p in range(2):
                hops[p, s, core, l].start()

    def forward_start(s):
        for p in range(2):
            hop_all[p, s].wait_recv()
        for core in range(2):
            for l in range(2):
                for p in range(2):
                    forwards[p, s, core, l].start()

    def project(low, high):
        for i in range(low, high):
            taken = rt.at[pl.ds(i * rows, rows)]
            pltpu.make_async_copy(taken, taken, right_sem.at[i]).wait()
            vec_in[i].wait()
            term = lax.dot_general(
                rt[pl.ds(i * rows, rows), :],
                win[pl.ds(HALO + i * rows, rows), :],
                (((0,), (0,)), ((), ())),
                preferred_element_type=F32,
            )
            if i == 0:
                pacc[...] = term
            else:
                pacc[...] += term

    project(0, EARLY)
    pl.semaphore_wait(barrier, len(partners))
    hop_start(pieces)
    near_in.start()
    project(EARLY, STEPS)
    for l in range(2):
        for zz in range(4):
            part[zz, l] = pacc[pl.ds(l * RB + zz * 32, 32), :].astype(BF)
    ways = (dev(at_z(zp), yh, k), dev(at_z(zm), yh, k))
    nexts = (zp, zm)
    lasts = (zm, zp)
    halves = (pl.ds(0, 16), pl.ds(16, 16))
    z_hop = []
    z_out = []
    z_fwd = []
    for d in range(2):
        z_hop.append(
            rcopy(part.at[zo, :, halves[d]], zrelay.at[d], z_s.at[0, d], z_r.at[0, d], ways[d])
        )
        z_out.append(rcopy(part.at[nexts[d]], zin.at[z], z_s.at[1, d], z_r.at[1, d], ways[d]))
        z_fwd.append(
            rcopy(
                zrelay.at[d], zin.at[lasts[d], :, halves[d]], z_s.at[2, d], z_r.at[2, d], ways[d]
            )
        )
    for copy in z_hop + z_out:
        copy.start()

    near_base = pl.multiple_of((1 - yl) * (HALO + M), HALO)
    far_base = pl.multiple_of(yl * (HALO + M), HALO)
    edge = jnp.logical_and(r > 0, r < 31)
    relays = jnp.logical_and(flip > 0, flip < 31)
    far_out = rcopy(
        vec.at[pl.ds(yl * (M - HALO) + (2 * yh + k) * QUARTER, QUARTER)],
        far_rows,
        far_s.at[0],
        far_r.at[0],
        dev((r + 30 + 4 * yl) % 32, yh, k),
    )
    near_halo = []
    far_halo = []
    near_share = []
    far_share = []
    for p in range(2):
        half = k * (HALO // 2) + p * sum(SPLIT[0])
        for i in range(2):
            mine = half + i * SPLIT[p][0]
            near_halo.append(
                rcopy(
                    vec.at[pl.ds((1 - yl) * (M - HALO) + mine, SPLIT[p][i])],
                    win.at[pl.ds(far_base + mine, SPLIT[p][i])],
                    near_s.at[p, i],
                    near_r.at[p, i],
                    dev(flip, highs[p], k),
                )
            )
        place = win.at[pl.ds(near_base + half, sum(SPLIT[p]))]
        near_share.append(rcopy(place, place, share_s.at[0, p], share_r.at[0, p], other))
        far_halo.append(
            rcopy(
                far_rows,
                win.at[pl.ds(near_base + (2 * yh + k) * QUARTER, QUARTER)],
                halo_s.at[p],
                halo_r.at[p],
                dev(flip, highs[p], k),
            )
        )
        place = win.at[pl.ds(far_base + (2 * highs[p] + k) * QUARTER, QUARTER)]
        far_share.append(rcopy(place, place, share_s.at[1, p], share_r.at[1, p], other))

    for copy in swaps + left_in:
        copy.start()

    nt[:, NNZ] = jnp.zeros((TILES, B, B), BF)
    near_in.wait()

    def assemble(w, carry):
        for t in range(TILES):
            place = jnp.int32(NNZ)
            for j in range(NNZ):
                place = jnp.where(cols[t, j] == w, j, place)
            dense[pl.ds(t * B, B), pl.ds(pl.multiple_of(w * B, B), B)] = nt[t, place]
        return carry

    lax.fori_loop(0, WINDOW, assemble, 0)
    for d in range(2):
        z_hop[d].wait_recv()
        z_fwd[d].start()

    def near_part(first, depth, low, high, initial=False):
        def columns(i, carry):
            here = pl.ds(pl.multiple_of(i * B, B), B)
            term = jnp.dot(
                dense[:, pl.ds(first, depth)],
                win[pl.ds(first, depth), here],
                preferred_element_type=F32,
            )
            if initial:
                acc[:, here] = term
            else:
                acc[:, here] += term
            return carry

        lax.fori_loop(low, high, columns, 0)

    done = [0]

    def advance(count):
        while count > 0:
            slab, low = divmod(done[0], 4)
            high = min(4, low + count)
            near_part(HALO + slab * 1024, 1024, low, high, slab == 0)
            done[0] += high - low
            count -= high - low

    advance(PLAN[0])

    for copy in z_out + z_fwd:
        copy.wait_recv()
    for l in range(2):
        base = pl.multiple_of(l * RB + z * 32, 32)
        total = pacc[pl.ds(base, 32), :]
        for j in range(1, 4):
            total = total + zin[(z + j) % 4, l].astype(F32)
        for low in range(2):
            xsend[l, low] = total[low * 16 : low * 16 + 16].astype(BF)

    for low in (1 - yl, yl):
        for l, plane, place in ((0, x2, xpar), (0, x3, xpar), (1, x1, 2)):
            rcopy(
                xsend.at[l, low],
                xin.at[place, yl],
                x_s.at[0],
                x_r.at[0],
                dev(plane * 8 + z * 2 + low, yh, k),
            ).start()
    x_all = rcopy(xin, xin, x_s.at[0], x_r.at[0], dev(at_x(x1), yh, k))
    for p in range(2):
        near_halo[2 * p].start()

    @pl.when(edge)
    def _():
        far_out.start()

    advance(PLAN[1])
    x_all.wait_recv()
    first = xin[0, 0].astype(F32) + xin[0, 1].astype(F32)
    first = first + (xin[1, 0].astype(F32) + xin[1, 1].astype(F32))
    coeff[k, 0, yh, z, yl] = first.astype(BF)
    coeff[k, 1, yh, z, yl] = (xin[2, 0].astype(F32) + xin[2, 1].astype(F32)).astype(BF)

    mine = coeff.at[k, :, yh, z, yl]
    g_out = [
        rcopy(mine, mine, g_s.at[i], g_r.at[i], target)
        for i, target in enumerate((dev(flip, yh, k), dev(flip, oh, k), dev(r, oh, k)))
    ]
    for i in (2, 0, 1):
        g_out[i].start()

    for p in range(2):
        near_halo[2 * p + 1].start()
    advance(PLAN[2])

    @pl.when(relays)
    def _():
        far_out.wait_recv()
        for copy in far_halo:
            copy.start()

    forward_start(0)
    advance(16 - done[0])
    for copy in g_out:
        copy.wait_recv()

    def level(l, zz):
        return coeff.at[k, l, :, zz]

    def ring_copy(l, zz, d, i):
        return rcopy(level(l, zz), level(l, zz), ring_s.at[d, i], ring_r.at[d, i], ways[d])

    ring = [
        [ring_copy(d, z, d, 0), ring_copy(1 - d, z, d, 1), ring_copy(d, lasts[d], d, 2)]
        for d in range(2)
    ]

    def core_start(l, zz):
        rcopy(level(l, zz), level(l, zz), core_s.at[0], core_r.at[0], other).start()

    core_out = rcopy(coeff.at[k], coeff.at[k], core_s.at[0], core_r.at[0], other)
    for i in range(2):
        for d in range(2):
            ring[d][i].start()
    for l in range(2):
        core_start(l, z)
    forward_start(1)
    for copy in near_halo:
        copy.wait_recv()
    for copy in near_share:
        copy.start()
    for d in range(2):
        ring[d][0].wait_recv()
        ring[d][2].start()
        core_start(d, lasts[d])

    @pl.when(edge)
    def _():
        for copy in far_halo:
            copy.wait_recv()
        for copy in far_share:
            copy.start()

    for copy in near_share:
        copy.wait_recv()
    near_part(near_base, HALO, 0, 4)
    for d in range(2):
        ring[d][1].wait_recv()
        core_start(1 - d, lasts[d])
    for d in range(2):
        ring[d][2].wait_recv()
        core_start(d, zo)

    @pl.when(edge)
    def _():
        for copy in far_share:
            copy.wait()

    @pl.when(jnp.logical_not(edge))
    def _():
        win[pl.ds(far_base, HALO), :] = jnp.zeros((HALO, N), BF)

    near_part(far_base, HALO, 0, 4)

    def far_part(chips, low, count, target):
        blocks = [(a, l, h) for a in range(2) for l in range(2) for h in chips]

        def columns(i, carry):
            here = pl.ds(pl.multiple_of(i * B, B), B)
            basis = jnp.concatenate([left[a, l, h, pl.ds(low, count)] for a, l, h in blocks], axis=1)
            weights = jnp.concatenate(
                [coeff[a, l, h, :, :, :, here].reshape(RB, B) for a, l, h in blocks], axis=0
            )
            term = jnp.dot(basis, weights, preferred_element_type=F32)
            total = acc[pl.ds(low, count), here] + term
            target[pl.ds(low, count), here] = total.astype(target.dtype)
            return carry

        lax.fori_loop(0, N // B, columns, 0)

    for copy in left_in:
        copy.wait()
    for copy in swaps:
        copy.wait_recv()
    core_out.wait_recv()
    far_part((yh,), 0, ROWS, acc)
    for core in range(2):
        arrival(0, core).wait_recv()
    far_part((oh,), *BLOCKS[0], out)
    for core in range(2):
        arrival(1, core).wait_recv()
    far_part((oh,), *BLOCKS[1], out)

    for copy in (
        list(hop_all.values())
        + list(fwd_all.values())
        + z_hop
        + z_out
        + z_fwd
        + [x_all]
        + g_out
        + ring[0]
        + ring[1]
        + [core_out]
        + swaps
        + near_halo
        + near_share
    ):
        copy.wait_send()

    @pl.when(edge)
    def _():
        far_out.wait_send()

    @pl.when(relays)
    def _():
        for copy in far_halo:
            copy.wait_send()


def per_device(vectors, near_tiles, near_cols, left_one, right_one, left_two, right_two):
    hbm = pl.BlockSpec(memory_space=pltpu.HBM)
    counts = [
        (STEPS,),
        (STEPS,),
        (3,),
        (2, 2),
        (2, 2),
        (2, 2),
        (2, 2),
        (2,),
        (2,),
        (1,),
        (1,),
        (2, 2),
        (2, 2),
        (2,),
        (2,),
        (2, 2),
        (2, 2),
        (3, 2),
        (3, 2),
        (1,),
        (1,),
        (3,),
        (3,),
        (2, 3),
        (2, 3),
        (1,),
        (1,),
    ]
    return pl.pallas_call(
        kernel,
        out_shape=pltpu.VMEM((ROWS, N), BF),
        in_specs=[pl.BlockSpec(memory_space=pltpu.SMEM)] + [hbm] * 6,
        out_specs=pl.BlockSpec(memory_space=pltpu.VMEM),
        scratch_shapes=[
            pltpu.VMEM((WINDOW * B, N), BF),
            pltpu.VMEM((TILES, NNZ + 1, B, B), BF),
            pltpu.VMEM((ROWS, WINDOW * B), BF),
            pltpu.VMEM((M, 2 * RB), BF),
            pltpu.VMEM((2 * RB, N), F32),
            pltpu.VMEM((4, 2, 32, N), BF),
            pltpu.VMEM((4, 2, 32, N), BF),
            pltpu.VMEM((2, 2, 16, N), BF),
            pltpu.VMEM((2, 2, 16, N), BF),
            pltpu.VMEM((3, 2, 16, N), BF),
            pltpu.VMEM((2, 2, 2, 4, 2, 16, N), BF),
            pltpu.VMEM((2, 2, 2, ROWS, RB), BF),
            pltpu.VMEM((2, 2, 2, HALF, RB), BF),
            pltpu.VMEM((QUARTER, N), BF),
            pltpu.VMEM((ROWS, N), F32),
        ]
        + [pltpu.SemaphoreType.DMA(shape) for shape in counts],
        compiler_params=pltpu.CompilerParams(
            collective_id=0, has_side_effects=True, vmem_limit_bytes=54 * 1024 * 1024
        ),
    )(near_cols, vectors, near_tiles, left_one, left_two, right_one, right_two)


def solution(mesh):
    placed = (
        P("rows", None),
        P(("rows", "cols"), None, None, None),
        P(("rows", "cols"), None),
        P("rows", "cols"),
        P("rows", "cols"),
        P("rows", "cols"),
        P("rows", "cols"),
    )
    return jax.shard_map(
        per_device, mesh=mesh, in_specs=placed, out_specs=P(("rows", "cols"), None), check_vma=False
    )
```
